32 devices in a mesh: groups: 2 (over y), span: 4 (over z), head: 4 (over x, core).
Axes of the slice: x: 2, y: 2, z: 4, core: 2. Of those that a mesh axis runs over, the one named last changes fastest.
Arguments:
- query_rows: bfloat16 [2048, 6144], P(('groups', 'span', 'head')), parts along dimension 0, may hold values from -6 to 6
- key_rows: bfloat16 [2048, 1024], P(('groups', 'span', 'head')), parts along dimension 0, may hold values from -6 to 6
- value_rows: bfloat16 [2048, 1024], P(('groups', 'span', 'head')), parts along dimension 0, may hold values from -6 to 6
- frame_counts: int32 [16], P('groups'), parts along dimension 0, may hold values from 1 to 4, as said below
- noise_levels: int32 [16], P('groups'), parts along dimension 0, may hold values from 0 to 63
- span_mask: int32 [16, 8], P('groups'), parts along dimension 0, may hold values from 0 to 1, as said below
- level_gate: bfloat16 [64, 6144], P(None, 'head'), may hold values from 0.19921875 to 1.796875
Outputs:
- attended: bfloat16 [2048, 6144], P(('groups', 'span', 'head')), parts along dimension 0
The draws below stay inside these ranges and needn't reach their ends.
There are 2 independent parts, one for each index of `groups`. The reference program is written for one: setup_inputs(seed, part) draws one part's arguments, and reference() takes and returns one part's arrays. A program takes and returns all parts, laid end to end along the dimension named above; an argument that names none is the same for every part. Nothing has to cross between parts.
Inputs may be any that keep to these rules, and one draw needn't show every extreme that they name: `frame_counts`: each span holds at least one frame, and some span holds exactly 4. span_mask[c, c] = 1 for every span, span_mask[c, e] = 0 for e > c, entries below the diagonal are 0 or 1.
All inputs are finite; a program needn't handle non-finite values.
Results may differ from the reference program's by a relative error of at most 0.0033.
Values may be sent and summed in bfloat16 or wider, within the bound.
No kernel may reach another device: no remote copies, remote signals or barrier semaphores. Data moves between devices by JAX's collectives and lax.ppermute only.
A program may use at most 64 MiB of HBM per device.

```python
import math
import jax
import jax.numpy as jnp
from jax import lax

HEADS = 48
KV_HEADS = 8
HD = 128
D = 6144
FRAME_TOK = 32
FMAX = 4
CT = 128
SPANS = 8
ROWS = 1024
LEVELS = 64


def draw_query_rows(key, part):
    return jnp.clip(1.7 * jax.random.normal(jax.random.fold_in(key, 5), (ROWS, D), jnp.float32), -6.0, 6.0).astype(jnp.bfloat16)


def draw_key_rows(key, part):
    return jnp.clip(1.7 * jax.random.normal(jax.random.fold_in(key, 6), (ROWS, KV_HEADS * HD), jnp.float32), -6.0, 6.0).astype(jnp.bfloat16)


def draw_frame_counts(key, part):
    frame_draw = jax.random.randint(jax.random.fold_in(key, 11), (SPANS,), 1, FMAX + 1, jnp.int32)
    busiest = jax.random.randint(jax.random.fold_in(key, 12), (), 0, SPANS, jnp.int32)
    return jnp.where(jnp.arange(SPANS, dtype=jnp.int32) == busiest, jnp.int32(FMAX), frame_draw).astype(jnp.int32)


def draw_span_mask(key, part):
    coin_flip = jax.random.randint(jax.random.fold_in(key, 13), (SPANS, SPANS), 0, 4, jnp.int32)
    row_index = jnp.arange(SPANS, dtype=jnp.int32)[:, None]
    col_index = jnp.arange(SPANS, dtype=jnp.int32)[None, :]
    below = jnp.where(col_index < row_index, (coin_flip > 0).astype(jnp.int32), 0)
    return jnp.where(col_index == row_index, 1, below).astype(jnp.int32)


def set_ends(array, stream_key, smallest, top_value):
    shape = array.shape
    index_at = [jax.random.randint(jax.random.fold_in(stream_key, axis), (), 0, shape[axis]) for axis in range(len(shape))]
    array = array.at[tuple(index_at)].set(smallest)
    longest = shape.index(max(shape))
    index_at[longest] = (index_at[longest] + 1) % shape[longest]
    return array.at[tuple(index_at)].set(top_value)


def block_levels(rng, shape, cuts, least, top_value):
    def one(dim, shards_of):
        heights = jax.random.uniform(jax.random.fold_in(jax.random.fold_in(rng, 6), dim), (shards_of,), jnp.float32, least / len(cuts), top_value / len(cuts))
        return jnp.repeat(jnp.exp(heights), shape[dim] // shards_of).reshape((-1,) + (1,) * (len(shape) - dim - 1))

    gain = one(*cuts[0])
    for cut in cuts[1:]:
        gain = gain * one(*cut)
    return gain


def scatter_about(rng, extent, scale, most, shards=(), held_as=jnp.bfloat16):
    level = block_levels(rng, extent, shards, -0.22, 0.18) if shards else 1.0
    values = jax.random.normal(rng, extent, jnp.float32) * scale * level
    return jnp.minimum(jnp.maximum(values, -most), most).astype(held_as)


def setup_inputs(seed: int = 0, part: int = 0) -> dict:
    key_of = jax.random.split(jax.random.key(seed), 8)
    part_keys = jax.random.split(jax.random.fold_in(key_of[7], part), 8)
    return {
        "query_rows": draw_query_rows(jax.random.fold_in(jax.random.fold_in(key_of[7], part), 71), part),
        "key_rows": draw_key_rows(jax.random.fold_in(jax.random.fold_in(key_of[7], part), 71), part),
        "value_rows": scatter_about(part_keys[2], (ROWS, KV_HEADS * HD), 1.0, 6.0, ((0, 16),)),
        "frame_counts": draw_frame_counts(jax.random.fold_in(jax.random.fold_in(key_of[7], part), 71), part),
        "noise_levels": set_ends(jax.random.randint(part_keys[4], (SPANS,), 0, LEVELS), jax.random.fold_in(part_keys[4], 1), 0, LEVELS - 1).astype(jnp.int32),
        "span_mask": draw_span_mask(jax.random.fold_in(jax.random.fold_in(key_of[7], part), 71), part),
        "level_gate": jnp.clip(0.19921875 + 1.5976562 * jax.random.uniform(key_of[6], (LEVELS, D), jnp.float32) ** block_levels(key_of[6], (LEVELS, D), ((1, 4),), -0.2, 0.2), 0.19921875, 1.796875).astype(jnp.bfloat16),
    }


def reference(query_rows, key_rows, value_rows, frame_counts, noise_levels, span_mask, level_gate):
    total_rows = query_rows.shape[0]
    span_count = total_rows // CT
    group_size = HEADS // KV_HEADS
    score_scale = 1.0 / math.sqrt(HD)
    position = jnp.arange(CT, dtype=jnp.int32)
    live_rows = position[None, :] < (frame_counts * FRAME_TOK)[:, None]
    live_flat = live_rows.reshape(-1)
    key_heads = key_rows.reshape(total_rows, KV_HEADS, HD).astype(jnp.float32)
    value_heads = value_rows.reshape(total_rows, KV_HEADS, HD).astype(jnp.float32)

    def one_span(span_index):
        mask_row = lax.dynamic_index_in_dim(span_mask, span_index, 0, keepdims=False)
        usable = (jnp.repeat(mask_row, CT, total_repeat_length=total_rows) > 0) & live_flat
        queries = lax.dynamic_slice_in_dim(query_rows, span_index * CT, CT, 0)
        queries = queries.reshape(CT, KV_HEADS, group_size, HD).astype(jnp.float32)

        def one_head(head_index):
            query_head = lax.dynamic_index_in_dim(queries, head_index, 1, keepdims=False)
            key_head = lax.dynamic_index_in_dim(key_heads, head_index, 1, keepdims=False)
            value_head = lax.dynamic_index_in_dim(value_heads, head_index, 1, keepdims=False)
            scores = jnp.einsum('qgd,kd->gqk', query_head, key_head) * score_scale
            masked = jnp.where(usable[None, None, :], scores, -jnp.inf)
            row_max = lax.optimization_barrier(jnp.max(masked, axis=2, keepdims=True))
            exponent = jnp.exp(masked - row_max)
            denominator = lax.optimization_barrier(jnp.sum(exponent, axis=2))
            weights = lax.optimization_barrier(exponent.astype(jnp.bfloat16)).astype(jnp.float32)
            numerator = jnp.einsum('gqk,kd->qgd', weights, value_head)
            return numerator / jnp.transpose(denominator)[:, :, None]
        outputs = lax.map(one_head, jnp.arange(KV_HEADS, dtype=jnp.int32))
        outputs = jnp.transpose(outputs, (1, 0, 2, 3)).reshape(CT, KV_HEADS * group_size * HD)
        level_index = lax.dynamic_index_in_dim(noise_levels, span_index, 0, keepdims=False)
        gate_row = lax.dynamic_index_in_dim(level_gate, level_index, 0, keepdims=False).astype(jnp.float32)
        query_live = lax.dynamic_index_in_dim(live_rows, span_index, 0, keepdims=False)
        result = jnp.where(query_live[:, None], outputs * gate_row[None, :], jnp.float32(0.0))
        return result.astype(jnp.bfloat16)
    blocks = lax.map(one_span, jnp.arange(span_count, dtype=jnp.int32))
    return blocks.reshape(total_rows, KV_HEADS * group_size * HD)
```

```python
import functools
import math

import jax
import jax.numpy as jnp
from jax import lax
from jax.experimental import pallas as pl
from jax.experimental.pallas import tpu as pltpu
from jax.sharding import PartitionSpec as P

HD = 128
FRAME_TOK = 32
CT = 128
KV_HEADS = 8
CORES = 2
NEG = -1e30
LOG2E = math.log2(math.e)


def attend_kernel(pieces, first, last, sizes, *refs):
    x_chips, rows_chip = sizes
    rows = rows_chip // CORES
    refs = list(refs)
    frames_ref, mask_ref, where_ref, q_own, q_other = refs[:5]
    del refs[:5]
    kv_refs = [refs.pop(0) for _ in pieces]
    if not first:
        stat_in, acc_in = refs.pop(0), refs.pop(0)
    if last:
        gate_ref, out_own, out_other = refs.pop(0), refs.pop(0), refs.pop(0)
    else:
        stat_out, acc_out = refs.pop(0), refs.pop(0)
    (bias_ref,) = refs
    z, head = where_ref[0], where_ref[1]
    x, core = head // CORES, head % CORES
    own_rows = (z * x_chips + x) * rows_chip
    own_span = own_rows // CT
    kv_cols = kv_refs[0].shape[1] // 2
    kv_heads = kv_cols // HD
    group = q_own.shape[1] // kv_cols

    slot = lax.broadcasted_iota(jnp.int32, (rows_chip, HD), 0)
    slot = lax.rem(slot + core * rows, rows_chip)
    for index, (up, side) in enumerate(pieces):
        source_z = z - up
        source_x = lax.rem(x - side + x_chips, x_chips)
        start = jnp.maximum((source_z * x_chips + source_x) * rows_chip, 0)
        span = start // CT
        there = jnp.logical_and(source_z >= 0, mask_ref[own_span, span] > 0)
        live = jnp.where(there, frames_ref[span] * FRAME_TOK - lax.rem(start, CT), 0)
        bias_ref[index * rows_chip : (index + 1) * rows_chip, :] = jnp.where(slot < live, 0.0, NEG)

    scale = LOG2E / math.sqrt(HD)
    if last:
        live_own = frames_ref[own_span] * FRAME_TOK - lax.rem(own_rows, CT)
        row = lax.broadcasted_iota(jnp.int32, (rows, HD), 0)
        own_live = row + core * rows < live_own
        other_live = row + (1 - core) * rows < live_own
    for g in range(kv_heads):
        cols = slice(g * HD, (g + 1) * HD)
        vcols = slice(kv_cols + g * HD, kv_cols + (g + 1) * HD)
        keys = jnp.concatenate([r[:, cols] for r in kv_refs], axis=0)
        values = jnp.concatenate([r[:, vcols] for r in kv_refs], axis=0)
        for pair in range(0, group, 2):
            heads = [g * group + pair + i for i in range(2)]
            queries = jnp.concatenate(
                [r[:, h * HD : (h + 1) * HD] for h in heads for r in (q_own, q_other)], axis=0
            )
            width = 2 * rows_chip
            lanes = slice(pair * rows_chip, pair * rows_chip + width)
            scores = lax.dot_general(
                keys, queries, (((1,), (1,)), ((), ())), preferred_element_type=jnp.float32
            )
            reps = -(-width // HD)
            bias = jnp.concatenate([bias_ref[...]] * reps, axis=1)[:, :width]
            scores = scores + bias
            top = jnp.max(scores, axis=0, keepdims=True)
            if not first:
                old_top = stat_in[g : g + 1, lanes]
                top = jnp.maximum(top, old_top)
            weights = jnp.exp2((scores - top) * scale)
            total = jnp.sum(weights, axis=0, keepdims=True)
            update = lax.dot_general(
                values,
                weights.astype(jnp.bfloat16),
                (((0,), (0,)), ((), ())),
                preferred_element_type=jnp.float32,
            )
            if not first:
                factor = jnp.exp2((old_top - top) * scale)
                total = total + factor * stat_in[kv_heads + g : kv_heads + g + 1, lanes]
                update = update + factor * acc_in[cols, lanes]
            if last:
                normed = update * (1.0 / total)
                for i, h in enumerate(heads):
                    hcols = slice(h * HD, (h + 1) * HD)
                    block = normed[:, i * rows_chip : (i + 1) * rows_chip].T
                    block = block * gate_ref[0:1, hcols]
                    out_own[:, hcols] = jnp.where(own_live, block[:rows], 0.0).astype(jnp.bfloat16)
                    out_other[:, hcols] = jnp.where(other_live, block[rows:], 0.0).astype(
                        jnp.bfloat16
                    )
            else:
                stat_out[g : g + 1, lanes] = top
                stat_out[kv_heads + g : kv_heads + g + 1, lanes] = total
                acc_out[cols, lanes] = update


def attend(pieces, kvs, state, gate, scalars, q_own, q_other, x_chips):
    first, last = state is None, gate is not None
    rows_chip = kvs[0].shape[0]
    rows, q_cols = q_own.shape
    kv_cols = kvs[0].shape[1] // 2
    kv_heads = kv_cols // HD
    lanes = q_cols // kv_cols * rows_chip
    smem = pl.BlockSpec(memory_space=pltpu.SMEM)
    vmem = pl.BlockSpec(memory_space=pltpu.VMEM)
    args = [*scalars, q_own, q_other, *kvs, *(state or ()), *((gate,) if last else ())]
    if last:
        outs = [jax.ShapeDtypeStruct((rows, q_cols), jnp.bfloat16)] * 2
    else:
        outs = [
            jax.ShapeDtypeStruct((2 * kv_heads, lanes), jnp.float32),
            jax.ShapeDtypeStruct((kv_heads * HD, lanes), jnp.float32),
        ]
    keys = len(pieces) * rows_chip
    return pl.pallas_call(
        functools.partial(attend_kernel, pieces, first, last, (x_chips, rows_chip)),
        out_shape=outs,
        in_specs=[smem] * 3 + [vmem] * (len(args) - 3),
        out_specs=[vmem] * 2,
        scratch_shapes=[pltpu.VMEM((keys, HD), jnp.float32)],
        compiler_params=pltpu.CompilerParams(vmem_limit_bytes=48 * 1024 * 1024),
        cost_estimate=pl.CostEstimate(
            flops=4 * keys * rows_chip * q_cols,
            transcendentals=keys * rows_chip * q_cols // HD,
            bytes_accessed=2 * rows_chip * q_cols + 4 * keys * kv_cols,
        ),
    )(*args)


def body(query_rows, key_rows, value_rows, frame_counts, noise_levels, span_mask, level_gate):
    z_chips = lax.axis_size("span")
    devices = lax.axis_size("head")
    x_chips = devices // CORES
    z = lax.axis_index("span")
    head = lax.axis_index("head")
    x, core = head // CORES, head % CORES
    rows, width = query_rows.shape
    half = width // CORES
    kv_half = key_rows.shape[1] // CORES
    rows_chip = rows * CORES
    spans_z = frame_counts.shape[0] // z_chips
    swap = [(h, h ^ 1) for h in range(devices)]

    def halves(array, cut):
        keep = lax.dynamic_slice_in_dim(array, core * cut, cut, 1)
        give = lax.dynamic_slice_in_dim(array, (1 - core) * cut, cut, 1)
        return keep, give

    def over_x(array, side):
        chips = [
            (s * CORES + c, (s + side) % x_chips * CORES + c)
            for s in range(x_chips)
            for c in range(CORES)
        ]
        return lax.ppermute(array, "head", chips)

    k_keep, k_give = halves(key_rows, kv_half)
    v_keep, v_give = halves(value_rows, kv_half)
    kv_got = lax.ppermute(jnp.concatenate([k_give, v_give], axis=1), "head", swap)
    own = jnp.concatenate([jnp.concatenate([k_keep, v_keep], axis=1), kv_got], axis=0)
    q_own, q_give = halves(query_rows, half)
    q_other = lax.ppermute(q_give, "head", swap)

    pieces, kvs = [(0, 0)], [own]
    held = own
    for side in range(1, x_chips):
        pieces.append((0, side))
        kvs.append(over_x(own, side))
    for up in range(1, z_chips):
        held = lax.ppermute(held, "span", [(s, s + 1) for s in range(up - 1, z_chips - 1)])
        pieces.append((up, 0))
        kvs.append(held)
        for side in range(1, x_chips):
            pieces.append((up, side))
            kvs.append(over_x(held, side))

    levels = lax.dynamic_slice_in_dim(noise_levels, z * spans_z, spans_z, 0)
    pick = (levels[:, None] == jnp.arange(level_gate.shape[0])[None, :]).astype(jnp.bfloat16)
    gate = jnp.dot(pick, level_gate, preferred_element_type=jnp.float32).astype(jnp.bfloat16)
    gate_got = lax.ppermute(gate, "head", swap)
    gate_pair = jnp.where(
        core == 0, jnp.stack([gate, gate_got], axis=1), jnp.stack([gate_got, gate], axis=1)
    )
    gate_all = jnp.stack([gate_pair] + [over_x(gate_pair, side) for side in range(1, x_chips)])
    order = lax.rem(x - jnp.arange(x_chips) + x_chips, x_chips)
    gate_all = gate_all[order]
    my_span = x * rows_chip // CT
    gate_row = lax.dynamic_index_in_dim(gate_all, my_span, 1, keepdims=False).reshape(1, width)
    gate_row = lax.dynamic_slice_in_dim(gate_row, core * half, half, 1).astype(jnp.float32)

    scalars = (frame_counts, span_mask, jnp.stack([z, head]))
    early = len(pieces) // 2
    run = functools.partial(
        attend, scalars=scalars, q_own=q_own, q_other=q_other, x_chips=x_chips
    )
    state = run(pieces[:early], kvs[:early], None, None)
    state = run(pieces[early:-1], kvs[early:-1], state, None)
    out_own, out_other = run(pieces[-1:], kvs[-1:], state, gate_row)
    out_got = lax.ppermute(out_other, "head", swap)
    return jnp.where(
        core == 0,
        jnp.concatenate([out_own, out_got], axis=1),
        jnp.concatenate([out_got, out_own], axis=1),
    )


def solution(mesh):
    tokens = P(("groups", "span", "head"), None)
    placed = (tokens, tokens, tokens, P("groups"), P("groups"), P("groups", None), P(None, "head"))
    return jax.shard_map(body, mesh=mesh, in_specs=placed, out_specs=tokens, check_vma=False)
```
